512 devices in a mesh: gx: 8 (over y), gy: 8 (over x, core), gz: 8 (over z).
Axes of the slice: x: 4, y: 8, z: 8, core: 2. Of those that a mesh axis runs over, the one named last changes fastest.
Arguments:
- bricks: bfloat16 [4096, 2, 128, 128], P(('gx', 'gy', 'gz')), may hold values from -6 to 6
- live: int32 [4096], P(('gx', 'gy', 'gz')), may hold values from 1 to 2, as said below
- shear: float32 [4, 2], replicated, may hold values from -1 to 1
- offsets: int32 [4096, 4, 2], P(('gx', 'gy', 'gz')), may hold values from -8 to 8
- absorb: bfloat16 [4096], P(('gx', 'gy', 'gz')), may hold values from 0.019897461 to 0.119628906
- color_gain: float32 [3], replicated, may hold values from 0.5 to 3
- color_bias: float32 [3], replicated, may hold values from -1 to 1
- targets: int32 [4096, 4], P(('gx', 'gy', 'gz')), may hold values from 0 to 1023, as said below
- order: int32 [4, 4096], P(None, ('gx', 'gy', 'gz')), may hold values from 0 to 4095, each once within a row
Outputs:
- image: float32 [1024, 4, 128, 128], P(('gx', 'gy', 'gz'))
The draws below stay inside these ranges and needn't reach their ends.
Inputs may be any that keep to these rules, and one draw needn't show every extreme that they name: Slices from live[b] on are empty; a device's rendering load can be up to twice another's. targets[b, v] = u has u mod 4 = v; tile u is owned by device u // 2 (devices counted in mesh order) and brick b by device b // 8, and both devices have the same gx index. A device sends at most 1 footprints to any one device; for each gx index some device receives 1 footprints from every device with that gx index. order[v] is a permutation of the bricks.
All inputs are finite; a program needn't handle non-finite values.
Results may differ from the reference program's by a relative error of at most 0.0016.
Values may be sent and summed in bfloat16 or wider, within the bound.
No kernel may reach another device: no remote copies, remote signals or barrier semaphores. Data moves between devices by JAX's collectives and lax.ppermute only.
A program may use at most 64 MiB of HBM per device.

```python
import math
import jax
import jax.numpy as jnp
from jax import lax

FOOT = 128
DEPTH = 2
BRICK_DEV = 8
VIEWS = 4
ROW = 64
CAP = 1
BRICKS = 4096
TILES = 1024


def draw_live(key, part):
    devices_all = BRICKS // BRICK_DEV
    ceiling = jax.random.randint(jax.random.fold_in(key, 11), (devices_all, 1), 1, DEPTH + 1)
    uniform_bits = jax.random.randint(jax.random.fold_in(key, 12), (devices_all, BRICK_DEV), 0, 1 << 20)
    counts_live = 1 + uniform_bits % ceiling
    chosen_brick = jax.random.randint(jax.random.fold_in(key, 13), (), 0, BRICKS)
    return counts_live.reshape(BRICKS).at[chosen_brick].set(DEPTH).astype(jnp.int32)


def draw_targets(key, part):
    groups_all = BRICKS // BRICK_DEV // ROW
    slot_span = ROW // 2 * CAP
    pick_count = 2 * BRICK_DEV
    slot_index = jnp.arange(slot_span)
    slot_owner = slot_index // CAP
    noise_bits = jax.random.randint(jax.random.fold_in(key, 21), (groups_all, ROW, 2, slot_span), 0, 1 << 20)
    busiest = jax.random.randint(jax.random.fold_in(key, 22), (groups_all, 1, 2, 1), 0, ROW // 2)
    scores = jnp.where(slot_owner == busiest, slot_index - slot_span, noise_bits * slot_span + slot_index)
    picked = jnp.argsort(scores, axis=-1)[..., :pick_count]
    mixing = jax.random.randint(jax.random.fold_in(key, 23), (groups_all, ROW, 2, pick_count), 0, 1 << 20) * pick_count + jnp.arange(pick_count)
    picked = jnp.take_along_axis(picked, jnp.argsort(mixing, axis=-1), axis=-1)
    parity = jnp.arange(2)[None, None, :, None]
    device_in_row = 2 * (picked // CAP) + parity
    row_start = (jnp.arange(groups_all) * ROW)[:, None, None, None]
    lower_view = jnp.arange(pick_count) % 2
    tile_number = 2 * (row_start + device_in_row) + lower_view
    tile_number = tile_number.reshape(groups_all, ROW, 2, BRICK_DEV, 2).transpose(0, 1, 3, 2, 4)
    return tile_number.reshape(BRICKS, 4).astype(jnp.int32)


def set_ends(drawn, stream_key, low, largest):
    longest = drawn.shape.index(max(drawn.shape))
    spots = []
    for shift in (0, 1):
        where = [jax.random.randint(jax.random.fold_in(stream_key, axis), (), 0, length) for axis, length in enumerate(drawn.shape)]
        where[longest] = (where[longest] + shift) % drawn.shape[longest]
        spots.append(tuple(where))
    return drawn.at[spots[0]].set(low).at[spots[1]].set(largest)


def level_of(own_key, dims, cuts, smallest, top_value):
    level, own = 1.0, jax.random.fold_in(own_key, 6)
    for dim, shards_of in cuts:
        heights = jnp.exp(jax.random.uniform(jax.random.fold_in(own, dim), (shards_of,), jnp.float32, smallest / len(cuts), top_value / len(cuts)))
        level = level * jnp.repeat(heights, dims[dim] // shards_of).reshape([-1 if axis == dim else 1 for axis in range(len(dims))])
    return level


def centred(key, shape, scale, bound, split=(), kind=jnp.bfloat16):
    result = scale * jax.random.normal(key, shape, jnp.float32)
    if split:
        result = result * level_of(key, shape, split, -0.22, 0.18)
    return jnp.clip(result, -bound, bound).astype(kind)


def setup_inputs(seed: int = 0) -> dict:
    seeds = jax.random.split(jax.random.key(seed), 10)
    return {
        "bricks": centred(seeds[0], (BRICKS, DEPTH, FOOT, FOOT), 1.0, 6.0, ((0, 512),)),
        "live": draw_live(jax.random.fold_in(seeds[9], 71), 0),
        "shear": jnp.clip(jax.random.uniform(seeds[2], (VIEWS, 2), jnp.float32, -1.0, 1.0), -1.0, 1.0),
        "offsets": set_ends(jax.random.randint(seeds[3], (BRICKS, VIEWS, 2), 0 - FOOT // 16, FOOT // 16 + 1), jax.random.fold_in(seeds[3], 1), 0 - FOOT // 16, (FOOT // 16 + 1) - 1).astype(jnp.int32),
        "absorb": jnp.clip(jnp.exp(math.log(0.119628906) - 1.7938024 * jax.random.uniform(seeds[4], (BRICKS,), jnp.float32) ** level_of(seeds[4], (BRICKS,), ((0, 512),), -0.2, 0.2)), 0.019897461, 0.119628906).astype(jnp.bfloat16),
        "color_gain": jnp.clip(jax.random.uniform(seeds[5], (3,), jnp.float32, 0.5, 3.0), 0.5, 3.0),
        "color_bias": jnp.clip(jax.random.uniform(seeds[6], (3,), jnp.float32, -1.0, 1.0), -1.0, 1.0),
        "targets": draw_targets(jax.random.fold_in(seeds[9], 71), 0),
        "order": jax.vmap(lambda own: jax.random.permutation(own, BRICKS))(jax.random.split(seeds[8], VIEWS)).reshape((VIEWS, BRICKS)).astype(jnp.int32),
    }


def interp_rows(shifted, extent):
    places = jnp.arange(extent, dtype=jnp.float32)
    spacing = places[:, None] - places[None, :] - shifted
    return jnp.maximum(0.0, 1.0 - jnp.abs(spacing)).astype(jnp.bfloat16)


def render(brick, live_count, absorb_rate, offset_pair, shear_pair, color_gain, color_bias):
    extent = brick.shape[-1]
    layers = brick.shape[0]
    offset_float = offset_pair.astype(jnp.float32)
    strength = absorb_rate.astype(jnp.float32)

    def advance(carry, inputs):
        colors, optical = carry
        layer, position = inputs
        raised = position.astype(jnp.float32) - jnp.float32(layers // 2)
        shifted = offset_float + raised * shear_pair
        across = interp_rows(shifted[0], extent)
        downward = interp_rows(shifted[1], extent)
        halfway = jnp.dot(across.astype(jnp.float32), layer.astype(jnp.float32), preferred_element_type=jnp.float32).astype(jnp.bfloat16)
        density = jnp.dot(halfway.astype(jnp.float32), downward.astype(jnp.float32).T, preferred_element_type=jnp.float32)
        thickness = jnp.where(position < live_count, strength * jax.nn.softplus(density), jnp.zeros_like(density))
        emitted = (1.0 - jnp.exp(-thickness))[None] * jax.nn.sigmoid(color_gain[:, None, None] * density[None] + color_bias[:, None, None])
        return (colors + jnp.exp(-optical)[None] * emitted, optical + thickness), None

    start = (jnp.zeros((3, extent, extent), jnp.float32), jnp.zeros((extent, extent), jnp.float32))
    (colors, optical), _ = lax.scan(advance, start, (brick, jnp.arange(layers, dtype=jnp.int32)))
    return colors.astype(jnp.bfloat16), optical.astype(jnp.bfloat16)


def reference(bricks, live, shear, offsets, absorb, color_gain, color_bias, targets, order):
    extent = bricks.shape[-1]
    color_image = jnp.zeros((TILES, 3, extent, extent), jnp.float32)
    depth_image = jnp.zeros((TILES, extent, extent), jnp.float32)
    for view in range(VIEWS):
        def visit(state, which):
            color_now, depth_now = state
            colors, optical = render(bricks[which], live[which], absorb[which], offsets[which, view], shear[view], color_gain, color_bias)
            target = targets[which, view].astype(jnp.int32)
            color_prior = lax.dynamic_index_in_dim(color_now, target, 0, keepdims=False)
            depth_prior = lax.dynamic_index_in_dim(depth_now, target, 0, keepdims=False)
            color_after = color_prior + jnp.exp(-depth_prior)[None] * colors.astype(jnp.float32)
            depth_after = depth_prior + optical.astype(jnp.float32)
            color_now = lax.dynamic_update_index_in_dim(color_now, color_after, target, 0)
            depth_now = lax.dynamic_update_index_in_dim(depth_now, depth_after, target, 0)
            return (color_now, depth_now), None

        sequence = jnp.argsort(order[view]).astype(jnp.int32)
        (color_image, depth_image), _ = lax.scan(visit, (color_image, depth_image), sequence)
    return jnp.concatenate([color_image, jnp.exp(-depth_image)[:, None]], axis=1)
```

```python
import jax
import jax.numpy as jnp
from jax import lax
from jax.experimental import pallas as pl
from jax.experimental.pallas import tpu as pltpu
from jax.sharding import PartitionSpec as P

ROWS = ("gy", "gz")
SMEM = pltpu.SMEM
VMEM = pltpu.VMEM


def pack_kernel(targets, order, offsets, live, absorb, bricks, send):
    slots = send.shape[0]
    views = targets.shape[1]
    body_rows = bricks.shape[1]
    lane = lax.broadcasted_iota(jnp.int32, (8, 128), 1)

    def clear(slot, _):
        send[slot, body_rows : body_rows + 8, :] = jnp.zeros((8, 128), send.dtype)
        return 0

    lax.fori_loop(0, slots, clear, 0)

    def one_brick(b, _):
        data = bricks[b]
        for v in range(views):
            tile = targets[b, v]
            slot = lax.rem(lax.div(tile, 2), slots)
            rank = order[v, b]
            fields = (
                (lax.rem(tile, 2) + 1).astype(jnp.float32),
                lax.div(rank, 64).astype(jnp.float32),
                lax.rem(rank, 64).astype(jnp.float32),
                offsets[b, v, 0].astype(jnp.float32),
                offsets[b, v, 1].astype(jnp.float32),
                live[b].astype(jnp.float32),
                absorb[b],
            )
            line = jnp.zeros((8, 128), jnp.float32)
            for at, value in enumerate(fields):
                line = jnp.where(lane == at, value, line)
            send[slot, 0:body_rows, :] = data
            send[slot, body_rows : body_rows + 8, :] = line.astype(send.dtype)
        return 0

    lax.fori_loop(0, bricks.shape[0], one_brick, 0)


def paint_kernel(
    shear, gain, bias, recv, image, feet, dens_a, dens_b, dens_c, dens_d, ints, reals,
    ints_s, reals_s, sems,
):
    slots = recv.shape[0]
    extent = recv.shape[2]
    layers = 2
    body_rows = layers * extent
    f32 = jnp.float32

    meta = jnp.max(recv[:, body_rows : body_rows + 8, :].astype(f32), axis=1)
    lane = lax.broadcasted_iota(jnp.int32, (slots, 128), 1)
    line = lax.broadcasted_iota(jnp.int32, (slots, 128), 0)
    line_f = line.astype(f32)

    def field(at):
        return jnp.sum(jnp.where(lane == at, meta, 0.0), axis=1, keepdims=True)

    def as_row(column, where_none=0.0):
        wide = jnp.broadcast_to(column, (slots, 128))
        row = jnp.sum(jnp.where(lane == line, wide, 0.0), axis=0, keepdims=True)
        if where_none:
            row = jnp.where(lane[0:1] < slots, row, where_none)
        return row

    def order_of(key):
        row = as_row(key, 1e9)
        place = jnp.sum(jnp.where(row < key, 1.0, 0.0), axis=1, keepdims=True)
        hit = place.astype(jnp.int32) == lane
        return jnp.sum(jnp.where(hit, line_f, 0.0), axis=0, keepdims=True)

    tile_1 = field(0)
    rank = field(1) * 64.0 + field(2)
    live = field(5)
    valid = tile_1 > 0.5
    index = line_f[:, 0:1]
    by_live = jnp.where(valid, live * 256.0 + index, 4096.0 + index)
    by_rank = jnp.where(valid, tile_1 * 4096.0 + rank, 16384.0 + index)
    ones = jnp.zeros((1, 128), f32)

    def count(mask):
        return ones + jnp.sum(jnp.where(mask, 1.0, 0.0), axis=0, keepdims=True)

    short = valid & (live < 1.5)
    rows_int = (
        order_of(by_live),
        order_of(by_rank),
        count(short),
        count(valid),
        count(valid & (tile_1 < 1.5)),
        as_row(tile_1),
    )
    for at, row in enumerate(rows_int):
        ints[at : at + 1, :] = row.astype(jnp.int32)
    for at, row in enumerate((as_row(field(3)), as_row(field(4)), as_row(field(6)))):
        reals[at : at + 1, :] = row
    copy_ints = pltpu.make_async_copy(ints, ints_s, sems.at[0])
    copy_reals = pltpu.make_async_copy(reals, reals_s, sems.at[1])
    copy_ints.start()
    copy_reals.start()
    image[...] = jnp.zeros_like(image)
    copy_ints.wait()
    copy_reals.wait()

    short_n = ints_s[2, 0]
    all_n = ints_s[3, 0]
    first_n = ints_s[4, 0]
    view_base = 2 * lax.rem(lax.axis_index("gz"), 2)
    apart = (
        lax.broadcasted_iota(jnp.int32, (extent, extent), 0)
        - lax.broadcasted_iota(jnp.int32, (extent, extent), 1)
    ).astype(f32)
    gains = [0.5 * gain[c] for c in range(3)]
    biases = [0.5 * bias[c] for c in range(3)]

    def density(slot, layer, out):
        view = view_base + ints_s[5, slot] - 1
        raised = f32(layer - layers // 2)
        sx = reals_s[0, slot] + raised * shear[view, 0]
        sy = reals_s[1, slot] + raised * shear[view, 1]
        across = jnp.maximum(0.0, 1.0 - jnp.abs(apart - sx)).astype(jnp.bfloat16)
        downward = jnp.maximum(0.0, 1.0 - jnp.abs(apart + sy)).astype(jnp.bfloat16)
        source = recv[slot, layer * extent : (layer + 1) * extent, :]
        halfway = jnp.dot(across, source, preferred_element_type=f32).astype(jnp.bfloat16)
        out[...] = jnp.dot(halfway, downward, preferred_element_type=f32)

    part = 32

    def shade(slot, dens):
        rate = reals_s[2, slot]
        for begin in range(0, extent, part):
            span = slice(begin, begin + part)
            colors = [None] * 3
            through = None
            for one in dens:
                d = one[span, :]
                thick = rate * jnp.log(1.0 + jnp.exp(d))
                pass_on = jnp.exp(-thick)
                half = 0.5 - 0.5 * pass_on
                if through is None:
                    through = pass_on
                    optical = thick
                else:
                    half = through * half
                    optical = optical + thick
                for c in range(3):
                    now = half * jnp.tanh(gains[c] * d + biases[c]) + half
                    colors[c] = now if colors[c] is None else colors[c] + now
            for c in range(3):
                feet[slot, c, span, :] = colors[c].astype(feet.dtype)
            feet[slot, 3, span, :] = optical.astype(feet.dtype)

    def render(begin, end, layer_count, bufs_a, bufs_b):
        def fill(at, bufs):
            slot = ints_s[0, jnp.minimum(at, end - 1)]
            for layer in range(layer_count):
                density(slot, layer, bufs[layer])

        def draw(at, bufs):
            shade(ints_s[0, jnp.minimum(at, end - 1)], bufs[:layer_count])

        @pl.when(end > begin)
        def _():
            fill(begin, bufs_a)

            def two(step, _):
                at = begin + 2 * step
                fill(at + 1, bufs_b)
                draw(at, bufs_a)
                fill(at + 2, bufs_a)
                draw(at + 1, bufs_b)
                return 0

            lax.fori_loop(0, lax.div(end - begin + 1, 2), two, 0)

    render(0, short_n, 1, (dens_a,), (dens_b,))
    render(short_n, all_n, 2, (dens_a, dens_c), (dens_b, dens_d))

    for tile in range(2):

        def lay(at, _):
            slot = ints_s[1, at]
            for begin in range(0, extent, part):
                span = slice(begin, begin + part)
                optical = image[tile, 3, span, :]
                through = jnp.exp(-optical)
                for c in range(3):
                    image[tile, c, span, :] += through * feet[slot, c, span, :].astype(f32)
                image[tile, 3, span, :] = optical + feet[slot, 3, span, :].astype(f32)
            return 0

        begin, end = (0, first_n) if tile == 0 else (first_n, all_n)
        lax.fori_loop(begin, end, lay, 0)
        image[tile, 3, :, :] = jnp.exp(-image[tile, 3, :, :])


def body(bricks, live, shear, offsets, absorb, color_gain, color_bias, targets, order):
    count, layers, extent, _ = bricks.shape
    slots = lax.axis_size(ROWS)
    rows = layers * extent
    smem = pl.BlockSpec(memory_space=SMEM)
    vmem = pl.BlockSpec(memory_space=VMEM)
    send = pl.pallas_call(
        pack_kernel,
        name="pack",
        out_shape=jax.ShapeDtypeStruct((slots, rows + 8, extent), jnp.bfloat16),
        in_specs=[smem] * 5 + [vmem],
        out_specs=vmem,
    )(
        targets,
        order,
        offsets,
        live,
        absorb.astype(jnp.float32),
        bricks.reshape(count, rows, extent),
    )
    recv = lax.all_to_all(send, ROWS, split_axis=0, concat_axis=0, tiled=True)
    square = VMEM((extent, extent), jnp.float32)
    return pl.pallas_call(
        paint_kernel,
        name="paint",
        out_shape=jax.ShapeDtypeStruct((2, 4, extent, extent), jnp.float32),
        in_specs=[smem] * 3 + [vmem],
        out_specs=vmem,
        scratch_shapes=[
            VMEM((slots, 4, extent, extent), jnp.bfloat16),
            square,
            square,
            square,
            square,
            VMEM((8, 128), jnp.int32),
            VMEM((8, 128), jnp.float32),
            SMEM((8, 128), jnp.int32),
            SMEM((8, 128), jnp.float32),
            pltpu.SemaphoreType.DMA((2,)),
        ],
    )(shear, color_gain, color_bias, recv)


def solution(mesh):
    whole = ("gx", "gy", "gz")
    placed = (
        P(whole, None, None, None),
        P(whole),
        P(),
        P(whole, None, None),
        P(whole),
        P(),
        P(),
        P(whole, None),
        P(None, whole),
    )
    return jax.shard_map(
        body,
        mesh=mesh,
        in_specs=placed,
        out_specs=P(whole, None, None, None),
        check_vma=False,
    )
```

```python
import jax
import jax.numpy as jnp
from jax import lax
from jax.experimental import pallas as pl
from jax.experimental.pallas import tpu as pltpu
from jax.sharding import PartitionSpec as P

SMEM = pltpu.SMEM
VMEM = pltpu.VMEM
F32 = jnp.float32
BF16 = jnp.bfloat16
META = 8
FIELDS = 8
PART = 32


def label_kernel(targets, order, offsets, live, absorb, bricks, block):
    views = targets.shape[0]
    rows = bricks.shape[1]
    slots = lax.axis_size("gy") * lax.axis_size("gz")
    lane = lax.broadcasted_iota(jnp.int32, (META, 128), 1)
    rates = absorb[...].astype(F32)
    spot = lax.broadcasted_iota(jnp.int32, rates.shape, 1)

    def one_brick(b, _):
        line = jnp.zeros((META, 128), F32)
        rate = jnp.sum(jnp.where(spot == b, rates, 0.0), axis=1, keepdims=True)
        for v in range(views):
            tile = targets[v, b]
            rank = order[v, b]
            fields = (
                (lax.rem(tile, 2) + 1).astype(F32),
                lax.div(rank, 64).astype(F32),
                lax.rem(rank, 64).astype(F32),
                offsets[v, 0, b].astype(F32),
                offsets[v, 1, b].astype(F32),
                live[b].astype(F32),
                rate,
                lax.rem(lax.div(tile, 2), slots).astype(F32),
            )
            for at, value in enumerate(fields):
                line = jnp.where(lane == v * FIELDS + at, value, line)
        block[b, 0:rows, :] = bricks[b]
        block[b, rows : rows + META, :] = line.astype(BF16)
        return 0

    lax.fori_loop(0, bricks.shape[0], one_brick, 0)


def pick_kernel(parts, *refs):
    blocks = refs[: len(parts)]
    send, names, names_s, sem = refs[len(parts) :]
    rows = send.shape[1] - META
    per = 1 + max(place for place, _ in parts)
    me = lax.axis_index("gz")
    planes = lax.axis_size("gz")
    start = 0
    for block in blocks:
        count = block.shape[0]
        lines = jnp.max(block[:, rows : rows + META, :].astype(F32), axis=1)
        names[start : start + count, :] = lines.astype(jnp.int32)
        start += count
    copy = pltpu.make_async_copy(names, names_s, sem)
    copy.start()
    for slot in range(send.shape[0]):
        send[slot, rows : rows + META, :] = jnp.zeros((META, 128), BF16)
    copy.wait()
    start = 0
    for block, (place, _) in zip(blocks, parts):

        def one_brick(b, _, block=block, place=place, start=start):
            for v in range(4):
                goal = names_s[start + b, v * FIELDS + FIELDS - 1]

                @pl.when(lax.rem(goal, planes) == me)
                def _():
                    slot = lax.div(goal, planes) * per + place
                    send[slot, 0:rows, :] = block[b, 0:rows, :]
                    line = block[b, rows : rows + META, :].astype(F32)
                    if v:
                        line = pltpu.roll(line, 128 - v * FIELDS, 1)
                    send[slot, rows : rows + META, :] = line.astype(BF16)

            return 0

        lax.fori_loop(0, block.shape[0], one_brick, 0)
        start += block.shape[0]


def as_row(column, count, empty=0.0):
    lane = lax.broadcasted_iota(jnp.int32, (count, 128), 1)
    line = lax.broadcasted_iota(jnp.int32, (count, 128), 0)
    wide = jnp.broadcast_to(column, (count, 128))
    row = jnp.sum(jnp.where(lane == line, wide, 0.0), axis=0, keepdims=True)
    if empty:
        row = jnp.where(lane[0:1] < count, row, empty)
    return row


def order_of(key, count):
    lane = lax.broadcasted_iota(jnp.int32, (count, 128), 1)
    line = lax.broadcasted_iota(jnp.int32, (count, 128), 0).astype(F32)
    row = as_row(key, count, 1e9)
    place = jnp.sum(jnp.where(row < key, 1.0, 0.0), axis=1, keepdims=True)
    hit = place.astype(jnp.int32) == lane
    return jnp.sum(jnp.where(hit, line, 0.0), axis=0, keepdims=True)


def plan(meta, first, ints, reals):
    count = meta.shape[0]
    lane = lax.broadcasted_iota(jnp.int32, (count, 128), 1)
    index = lax.broadcasted_iota(jnp.int32, (count, 1), 0).astype(F32)

    def field(at):
        return jnp.sum(jnp.where(lane == at, meta, 0.0), axis=1, keepdims=True)

    def total(mask):
        zero = jnp.zeros((1, 128), F32)
        return zero + jnp.sum(jnp.where(mask, 1.0, 0.0), axis=0, keepdims=True)

    tile_1 = field(0)
    rank = field(1) * 64.0 + field(2)
    live = field(5)
    valid = tile_1 > 0.5
    fresh = valid & (index > first - 0.5)
    by_live = jnp.where(fresh, live * 256.0 + index, 4096.0 + index)
    by_rank = jnp.where(valid, tile_1 * 4096.0 + rank, 16384.0 + index)
    rows = (
        order_of(by_live, count),
        order_of(by_rank, count),
        total(fresh & (live < 1.5)),
        total(fresh),
        total(valid),
        total(valid & (tile_1 < 1.5)),
        as_row(tile_1, count),
    )
    for at, row in enumerate(rows):
        ints[at : at + 1, :] = row.astype(jnp.int32)
    for at, row in enumerate((field(3), field(4), field(6))):
        reals[at : at + 1, :] = as_row(row, count)


def draw_all(shear, gain, bias, recv, first, feet, bufs, ints_s, reals_s):
    extent = recv.shape[2]
    layers = (recv.shape[1] - META) // extent
    view_base = 2 * lax.rem(lax.axis_index("gz"), 2)
    apart = (
        lax.broadcasted_iota(jnp.int32, (extent, extent), 0)
        - lax.broadcasted_iota(jnp.int32, (extent, extent), 1)
    ).astype(F32)
    gains = [0.5 * gain[c] for c in range(3)]
    biases = [0.5 * bias[c] for c in range(3)]

    def density(slot, layer, out):
        view = view_base + ints_s[6, slot] - 1
        raised = F32(layer - layers // 2)
        sx = reals_s[0, slot] + raised * shear[0, view]
        sy = reals_s[1, slot] + raised * shear[1, view]
        across = jnp.maximum(0.0, 1.0 - jnp.abs(apart - sx)).astype(BF16)
        downward = jnp.maximum(0.0, 1.0 - jnp.abs(apart + sy)).astype(BF16)
        source = recv[slot - first, layer * extent : (layer + 1) * extent, :]
        halfway = jnp.dot(across, source, preferred_element_type=F32).astype(BF16)
        out[...] = jnp.dot(halfway, downward, preferred_element_type=F32)

    def shade(slot, dens):
        rate = reals_s[2, slot]
        for begin in range(0, extent, PART):
            span = slice(begin, begin + PART)
            colors = [None] * 3
            through = None
            for one in dens:
                d = one[span, :]
                thick = rate * jnp.log(1.0 + jnp.exp(d))
                pass_on = jnp.exp(-thick)
                half = 0.5 - 0.5 * pass_on
                if through is None:
                    through = pass_on
                    optical = thick
                else:
                    half = through * half
                    optical = optical + thick
                for c in range(3):
                    now = half * jnp.tanh(gains[c] * d + biases[c]) + half
                    colors[c] = now if colors[c] is None else colors[c] + now
            for c in range(3):
                feet[slot, c, span, :] = colors[c].astype(BF16)
            feet[slot, 3, span, :] = optical.astype(BF16)

    def render(begin, end, layer_count, bufs_a, bufs_b):
        def fill(at, dens):
            slot = ints_s[0, jnp.minimum(at, end - 1)]
            for layer in range(layer_count):
                density(slot, layer, dens[layer])

        def draw(at, dens):
            shade(ints_s[0, jnp.minimum(at, end - 1)], dens[:layer_count])

        @pl.when(end > begin)
        def _():
            fill(begin, bufs_a)

            def two(step, _):
                at = begin + 2 * step
                fill(at + 1, bufs_b)
                draw(at, bufs_a)
                fill(at + 2, bufs_a)
                draw(at + 1, bufs_b)
                return 0

            lax.fori_loop(0, lax.div(end - begin + 1, 2), two, 0)

    short_n = ints_s[2, 0]
    fresh_n = ints_s[3, 0]
    render(0, short_n, 1, bufs[0:1], bufs[2:3])
    render(short_n, fresh_n, 2, bufs[0:2], bufs[2:4])


def render_kernel(shear, gain, bias, recv, feet, b0, b1, b2, b3, ints, reals, ints_s, reals_s, sems):
    rows = recv.shape[1] - META
    meta = jnp.max(recv[:, rows : rows + META, :].astype(F32), axis=1)
    plan(meta, 0, ints, reals)
    copies = [
        pltpu.make_async_copy(ints, ints_s, sems.at[0]),
        pltpu.make_async_copy(reals, reals_s, sems.at[1]),
    ]
    for copy in copies:
        copy.start()
    for copy in copies:
        copy.wait()
    draw_all(shear, gain, bias, recv, 0, feet, (b0, b1, b2, b3), ints_s, reals_s)


def paint_kernel(*refs):
    shear, gain, bias = refs[:3]
    (image, feet, b0, b1, b2, b3, lines, ints, reals, ints_s, reals_s, sems) = refs[-12:]
    middle = refs[3:-12]
    recv = middle[-1]
    done = len(middle) // 2
    extent = recv.shape[2]
    rows = recv.shape[1] - META
    first = 0
    meta_copies, feet_copies = [], []
    for group in range(done):
        old, old_feet = middle[2 * group], middle[2 * group + 1]
        count = old.shape[0]
        span = pl.ds(first, count)
        meta_copies.append(
            pltpu.make_async_copy(
                old.at[:, pl.ds(rows, META), :], lines.at[span], sems.at[2 * group + 2]
            )
        )
        feet_copies.append(
            pltpu.make_async_copy(old_feet, feet.at[span], sems.at[2 * group + 3])
        )
        first += count
    for copy in meta_copies + feet_copies:
        copy.start()
    lines[first : first + recv.shape[0]] = recv[:, rows : rows + META, :]
    image[...] = jnp.zeros_like(image)
    for copy in meta_copies:
        copy.wait()
    meta = jnp.max(lines[...].astype(F32), axis=1)
    plan(meta, first, ints, reals)
    copies = [
        pltpu.make_async_copy(ints, ints_s, sems.at[0]),
        pltpu.make_async_copy(reals, reals_s, sems.at[1]),
    ]
    for copy in copies:
        copy.start()
    for copy in copies:
        copy.wait()
    draw_all(shear, gain, bias, recv, first, feet, (b0, b1, b2, b3), ints_s, reals_s)
    for copy in feet_copies:
        copy.wait()

    all_n = ints_s[4, 0]
    first_n = ints_s[5, 0]
    for tile in range(2):

        def lay(at, _):
            slot = ints_s[1, at]
            for begin in range(0, extent, PART):
                span = slice(begin, begin + PART)
                optical = image[tile, 3, span, :]
                through = jnp.exp(-optical)
                for c in range(3):
                    image[tile, c, span, :] += through * feet[slot, c, span, :].astype(F32)
                image[tile, 3, span, :] = optical + feet[slot, 3, span, :].astype(F32)
            return 0

        begin, end = (0, first_n) if tile == 0 else (first_n, all_n)
        lax.fori_loop(begin, end, lay, 0)
        image[tile, 3, :, :] = jnp.exp(-image[tile, 3, :, :])


def body(bricks, live, shear, offsets, absorb, color_gain, color_bias, targets, order):
    count, layers, extent, _ = bricks.shape
    rows = layers * extent
    columns = lax.axis_size("gy")
    planes = lax.axis_size("gz")
    smem = pl.BlockSpec(memory_space=SMEM)
    vmem = pl.BlockSpec(memory_space=VMEM)
    here = pl.BlockSpec(memory_space=pl.ANY)
    square = VMEM((extent, extent), F32)
    tables = [
        square,
        square,
        square,
        square,
    ]
    small = [
        VMEM((8, 128), jnp.int32),
        VMEM((8, 128), F32),
        SMEM((8, 128), jnp.int32),
        SMEM((8, 128), F32),
    ]
    block = pl.pallas_call(
        label_kernel,
        name="label",
        out_shape=jax.ShapeDtypeStruct((count, rows + META, extent), BF16),
        in_specs=[smem] * 4 + [vmem] * 2,
        out_specs=vmem,
    )(
        targets.T,
        order,
        offsets.transpose(1, 2, 0),
        live,
        absorb.reshape(1, count),
        bricks.reshape(count, rows, extent),
    )

    def move(what, step):
        return lax.ppermute(what, "gz", [(z, (z + step) % planes) for z in range(planes)])

    def pick(parts, blocks):
        per = 1 + max(place for place, _ in parts)
        total = sum(b.shape[0] for b in blocks)
        return pl.pallas_call(
            lambda *refs: pick_kernel(parts, *refs),
            name="pick",
            out_shape=jax.ShapeDtypeStruct((columns * per, rows + META, extent), BF16),
            in_specs=[vmem] * len(blocks),
            out_specs=vmem,
            scratch_shapes=[
                VMEM((total, 128), jnp.int32),
                SMEM((total, 128), jnp.int32),
                pltpu.SemaphoreType.DMA,
            ],
            cost_estimate=pl.CostEstimate(flops=0, bytes_accessed=6_000_000, transcendentals=0),
        )(*blocks)

    def spread(what):
        return lax.all_to_all(what, "gy", split_axis=0, concat_axis=0, tiled=True)

    def render(recv):
        slots = recv.shape[0]
        return pl.pallas_call(
            render_kernel,
            name="render",
            out_shape=jax.ShapeDtypeStruct((slots, 4, extent, extent), BF16),
            in_specs=[smem] * 3 + [vmem],
            out_specs=vmem,
            scratch_shapes=tables + small + [pltpu.SemaphoreType.DMA((2,))],
            cost_estimate=pl.CostEstimate(flops=0, bytes_accessed=8_000_000, transcendentals=0),
        )(shear.T, color_gain, color_bias, recv)

    half = count // 2
    ups, downs = [block], [block]
    for _ in range(1, planes // 2):
        ups.append(move(ups[-1], 1))
        downs.append(move(downs[-1], -1))
    up_far = move(ups[-1][:half], 1)
    down_far = move(downs[-1][half:], -1)

    groups = (
        (((0, 0),), (block,)),
        (((0, 0), (1, 0)), (ups[1], downs[1])),
        (((0, 0), (1, 0)), (ups[2], downs[2])),
        (((0, 0), (1, 0), (2, 0), (2, 0)), (ups[3], downs[3], up_far, down_far)),
    )
    received = []
    for parts, blocks in groups:
        send = pick(parts, blocks)
        received.append(spread(send))
    slots = sum(r.shape[0] for r in received)
    middle = []
    for recv in received[:-1]:
        middle += [recv, render(recv)]
    return pl.pallas_call(
        paint_kernel,
        name="paint",
        out_shape=jax.ShapeDtypeStruct((2, 4, extent, extent), F32),
        in_specs=[smem] * 3 + [here] * len(middle) + [vmem],
        out_specs=vmem,
        scratch_shapes=[VMEM((slots, 4, extent, extent), BF16)]
        + tables
        + [VMEM((slots, META, 128), BF16)]
        + small
        + [pltpu.SemaphoreType.DMA((2 + len(middle),))],
    )(shear.T, color_gain, color_bias, *middle, received[-1])


def solution(mesh):
    whole = ("gx", "gy", "gz")
    placed = (
        P(whole, None, None, None),
        P(whole),
        P(),
        P(whole, None, None),
        P(whole),
        P(),
        P(),
        P(whole, None),
        P(None, whole),
    )

    return jax.shard_map(
        body,
        mesh=mesh,
        in_specs=placed,
        out_specs=P(whole, None, None, None),
        check_vma=False,
    )
```

```python
import jax
import jax.numpy as jnp
from jax import lax
from jax.experimental import pallas as pl
from jax.experimental.pallas import tpu as pltpu
from jax.sharding import PartitionSpec as P

SMEM = pltpu.SMEM
VMEM = pltpu.VMEM
F32 = jnp.float32
BF16 = jnp.bfloat16
META = 8
FIELDS = 8
PART = 32


def label_kernel(targets, order, offsets, live, absorb, bricks, block):
    views = targets.shape[0]
    rows = bricks.shape[1]
    slots = lax.axis_size("gy") * lax.axis_size("gz")
    lane = lax.broadcasted_iota(jnp.int32, (META, 128), 1)
    rates = absorb[...].astype(F32)
    spot = lax.broadcasted_iota(jnp.int32, rates.shape, 1)

    def one_brick(b, _):
        line = jnp.zeros((META, 128), F32)
        rate = jnp.sum(jnp.where(spot == b, rates, 0.0), axis=1, keepdims=True)
        for v in range(views):
            tile = targets[v, b]
            rank = order[v, b]
            fields = (
                (lax.rem(tile, 2) + 1).astype(F32),
                lax.div(rank, 64).astype(F32),
                lax.rem(rank, 64).astype(F32),
                offsets[v, 0, b].astype(F32),
                offsets[v, 1, b].astype(F32),
                live[b].astype(F32),
                rate,
                lax.rem(lax.div(tile, 2), slots).astype(F32),
            )
            for at, value in enumerate(fields):
                line = jnp.where(lane == v * FIELDS + at, value, line)
        block[b, 0:rows, :] = bricks[b]
        block[b, rows : rows + META, :] = line.astype(BF16)
        return 0

    lax.fori_loop(0, bricks.shape[0], one_brick, 0)


def pick_kernel(parts, *refs, per=None):
    blocks = refs[: len(parts)]
    send, names, names_s, sem = refs[len(parts) :]
    rows = send.shape[1] - META
    per = per or 1 + max(place for place, _ in parts)
    me = lax.axis_index("gz")
    planes = lax.axis_size("gz")
    start = 0
    for block in blocks:
        count = block.shape[0]
        lines = jnp.max(block[:, rows : rows + META, :].astype(F32), axis=1)
        names[start : start + count, :] = lines.astype(jnp.int32)
        start += count
    copy = pltpu.make_async_copy(names, names_s, sem)
    copy.start()
    for slot in range(send.shape[0]):
        send[slot, rows : rows + META, :] = jnp.zeros((META, 128), BF16)
    copy.wait()
    start = 0
    for block, (place, _) in zip(blocks, parts):

        def one_brick(b, _, block=block, place=place, start=start):
            for v in range(4):
                goal = names_s[start + b, v * FIELDS + FIELDS - 1]

                @pl.when(lax.rem(goal, planes) == me)
                def _():
                    slot = lax.div(goal, planes) * per + place
                    send[slot, 0:rows, :] = block[b, 0:rows, :]
                    line = block[b, rows : rows + META, :].astype(F32)
                    if v:
                        line = pltpu.roll(line, 128 - v * FIELDS, 1)
                    send[slot, rows : rows + META, :] = line.astype(BF16)

            return 0

        lax.fori_loop(0, block.shape[0], one_brick, 0)
        start += block.shape[0]


def add_kernel(place, per, block, _, send, fresh, names, names_s, sem, sems):
    pick_kernel(((0, 0),), block, fresh, names, names_s, sem)
    copies = [
        pltpu.make_async_copy(fresh.at[row], send.at[row * per + place], sems.at[row])
        for row in range(fresh.shape[0])
    ]
    for copy in copies:
        copy.start()
    for copy in copies:
        copy.wait()


def as_row(column, count, empty=0.0):
    lane = lax.broadcasted_iota(jnp.int32, (count, 128), 1)
    line = lax.broadcasted_iota(jnp.int32, (count, 128), 0)
    wide = jnp.broadcast_to(column, (count, 128))
    row = jnp.sum(jnp.where(lane == line, wide, 0.0), axis=0, keepdims=True)
    if empty:
        row = jnp.where(lane[0:1] < count, row, empty)
    return row


def order_of(key, count):
    lane = lax.broadcasted_iota(jnp.int32, (count, 128), 1)
    line = lax.broadcasted_iota(jnp.int32, (count, 128), 0).astype(F32)
    row = as_row(key, count, 1e9)
    place = jnp.sum(jnp.where(row < key, 1.0, 0.0), axis=1, keepdims=True)
    hit = place.astype(jnp.int32) == lane
    return jnp.sum(jnp.where(hit, line, 0.0), axis=0, keepdims=True)


def field_of(meta, at):
    lane = lax.broadcasted_iota(jnp.int32, meta.shape, 1)
    return jnp.sum(jnp.where(lane == at, meta, 0.0), axis=1, keepdims=True)


def total_of(mask):
    zero = jnp.zeros((1, 128), F32)
    return zero + jnp.sum(jnp.where(mask, 1.0, 0.0), axis=0, keepdims=True)


def index_of(meta):
    return lax.broadcasted_iota(jnp.int32, (meta.shape[0], 1), 0).astype(F32)


def plan_draw(meta, ints, reals):
    count = meta.shape[0]
    tile_1 = field_of(meta, 0)
    live = field_of(meta, 5)
    valid = tile_1 > 0.5
    index = index_of(meta)
    key = jnp.where(valid, live * 256.0 + index, 4096.0 + index)
    rows = (
        order_of(key, count),
        total_of(valid & (live < 1.5)),
        total_of(valid),
        as_row(tile_1, count),
    )
    for at, row in enumerate(rows):
        ints[at : at + 1, :] = row.astype(jnp.int32)
    for at, name in enumerate((3, 4, 6)):
        reals[at : at + 1, :] = as_row(field_of(meta, name), count)


def plan_lay(meta, ints):
    count = meta.shape[0]
    tile_1 = field_of(meta, 0)
    rank = field_of(meta, 1) * 64.0 + field_of(meta, 2)
    valid = tile_1 > 0.5
    key = jnp.where(valid, tile_1 * 4096.0 + rank, 16384.0 + index_of(meta))
    rows = (order_of(key, count), total_of(valid & (tile_1 < 1.5)), total_of(valid))
    for at, row in enumerate(rows):
        ints[at : at + 1, :] = row.astype(jnp.int32)


def draw_all(shear, gain, bias, recv, first, feet, bufs, ints_s, reals_s):
    extent = recv.shape[2]
    layers = (recv.shape[1] - META) // extent
    view_base = 2 * lax.rem(lax.axis_index("gz"), 2)
    apart = (
        lax.broadcasted_iota(jnp.int32, (extent, extent), 0)
        - lax.broadcasted_iota(jnp.int32, (extent, extent), 1)
    ).astype(F32)
    gains = [0.5 * gain[c] for c in range(3)]
    biases = [0.5 * bias[c] for c in range(3)]

    def density(slot, layer, out):
        view = view_base + ints_s[3, slot] - 1
        raised = F32(layer - layers // 2)
        sx = reals_s[0, slot] + raised * shear[0, view]
        sy = reals_s[1, slot] + raised * shear[1, view]
        across = jnp.maximum(0.0, 1.0 - jnp.abs(apart - sx)).astype(BF16)
        downward = jnp.maximum(0.0, 1.0 - jnp.abs(apart + sy)).astype(BF16)
        source = recv[slot, layer * extent : (layer + 1) * extent, :]
        halfway = jnp.dot(across, source, preferred_element_type=F32).astype(BF16)
        out[...] = jnp.dot(halfway, downward, preferred_element_type=F32)

    def shade(slot, dens):
        rate = reals_s[2, slot]
        for begin in range(0, extent, PART):
            span = slice(begin, begin + PART)
            colors = [None] * 3
            through = None
            for one in dens:
                d = one[span, :]
                thick = rate * jnp.log(1.0 + jnp.exp(d))
                pass_on = jnp.exp(-thick)
                half = 0.5 - 0.5 * pass_on
                if through is None:
                    through = pass_on
                    optical = thick
                else:
                    half = through * half
                    optical = optical + thick
                for c in range(3):
                    now = half * jnp.tanh(gains[c] * d + biases[c]) + half
                    colors[c] = now if colors[c] is None else colors[c] + now
            for c in range(3):
                feet[first + slot, c, span, :] = colors[c].astype(BF16)
            feet[first + slot, 3, span, :] = optical.astype(BF16)

    def render(begin, end, layer_count, bufs_a, bufs_b):
        def fill(at, dens):
            slot = ints_s[0, jnp.minimum(at, end - 1)]
            for layer in range(layer_count):
                density(slot, layer, dens[layer])

        def draw(at, dens):
            shade(ints_s[0, jnp.minimum(at, end - 1)], dens[:layer_count])

        @pl.when(end > begin)
        def _():
            fill(begin, bufs_a)

            def two(step, _):
                at = begin + 2 * step
                fill(at + 1, bufs_b)
                draw(at, bufs_a)
                fill(at + 2, bufs_a)
                draw(at + 1, bufs_b)
                return 0

            lax.fori_loop(0, lax.div(end - begin + 1, 2), two, 0)

    short_n = ints_s[1, 0]
    fresh_n = ints_s[2, 0]
    render(0, short_n, 1, bufs[0:1], bufs[2:3])
    render(short_n, fresh_n, 2, bufs[0:2], bufs[2:4])


def render_kernel(shear, gain, bias, recv, feet, b0, b1, b2, b3, ints, reals, ints_s, reals_s, sems):
    rows = recv.shape[1] - META
    meta = jnp.max(recv[:, rows : rows + META, :].astype(F32), axis=1)
    plan_draw(meta, ints, reals)
    copies = [
        pltpu.make_async_copy(ints, ints_s, sems.at[0]),
        pltpu.make_async_copy(reals, reals_s, sems.at[1]),
    ]
    for copy in copies:
        copy.start()
    for copy in copies:
        copy.wait()
    draw_all(shear, gain, bias, recv, 0, feet, (b0, b1, b2, b3), ints_s, reals_s)


def paint_kernel(*refs):
    shear, gain, bias = refs[:3]
    (image, feet, b0, b1, b2, b3, lines, recv, places, places_s) = refs[-15:-5]
    (ints, reals, ints_s, reals_s, sems) = refs[-5:]
    middle = refs[3:-15]
    last = middle[-1]
    done = len(middle) // 2
    extent = last.shape[2]
    rows = last.shape[1] - META
    meta_copies, feet_copies = [], []
    first = 0
    for group in range(done + 1):
        old = middle[2 * group]
        span = pl.ds(first, old.shape[0])
        meta_copies.append(
            pltpu.make_async_copy(
                old.at[:, pl.ds(rows, META), :], lines.at[span], sems.at[2 * group]
            )
        )
        if group < done:
            feet_copies.append(
                pltpu.make_async_copy(middle[2 * group + 1], feet.at[span], sems.at[2 * group + 1])
            )
            first += old.shape[0]
    bulk = pltpu.make_async_copy(last, recv, sems.at[2 * done + 1])
    for copy in meta_copies[::-1] + [bulk] + feet_copies:
        copy.start()
    draw_ints = pltpu.make_async_copy(ints, ints_s, sems.at[2 * done + 2])
    draw_reals = pltpu.make_async_copy(reals, reals_s, sems.at[2 * done + 3])
    lay_ints = pltpu.make_async_copy(places, places_s, sems.at[2 * done + 4])
    image[...] = jnp.zeros_like(image)
    meta_copies[-1].wait()
    plan_draw(jnp.max(lines[first:].astype(F32), axis=1), ints, reals)
    draw_ints.start()
    draw_reals.start()
    for copy in meta_copies[:-1]:
        copy.wait()
    plan_lay(jnp.max(lines[...].astype(F32), axis=1), places)
    lay_ints.start()
    draw_ints.wait()
    draw_reals.wait()
    bulk.wait()
    draw_all(shear, gain, bias, recv, first, feet, (b0, b1, b2, b3), ints_s, reals_s)
    for copy in feet_copies:
        copy.wait()
    lay_ints.wait()

    all_n = places_s[2, 0]
    first_n = places_s[1, 0]
    for tile in range(2):

        def lay(at, _):
            slot = places_s[0, at]
            for begin in range(0, extent, PART):
                span = slice(begin, begin + PART)
                optical = image[tile, 3, span, :]
                through = jnp.exp(-optical)
                for c in range(3):
                    image[tile, c, span, :] += through * feet[slot, c, span, :].astype(F32)
                image[tile, 3, span, :] = optical + feet[slot, 3, span, :].astype(F32)
            return 0

        begin, end = (0, first_n) if tile == 0 else (first_n, all_n)
        lax.fori_loop(begin, end, lay, 0)
        image[tile, 3, :, :] = jnp.exp(-image[tile, 3, :, :])


def body(bricks, live, shear, offsets, absorb, color_gain, color_bias, targets, order):
    count, layers, extent, _ = bricks.shape
    rows = layers * extent
    columns = lax.axis_size("gy")
    planes = lax.axis_size("gz")
    smem = pl.BlockSpec(memory_space=SMEM)
    vmem = pl.BlockSpec(memory_space=VMEM)
    here = pl.BlockSpec(memory_space=pl.ANY)
    square = VMEM((extent, extent), F32)
    tables = [
        square,
        square,
        square,
        square,
    ]
    small = [
        VMEM((8, 128), jnp.int32),
        VMEM((8, 128), F32),
        SMEM((8, 128), jnp.int32),
        SMEM((8, 128), F32),
    ]
    block = pl.pallas_call(
        label_kernel,
        name="label",
        out_shape=jax.ShapeDtypeStruct((count, rows + META, extent), BF16),
        in_specs=[smem] * 4 + [vmem] * 2,
        out_specs=vmem,
    )(
        targets.T,
        order,
        offsets.transpose(1, 2, 0),
        live,
        absorb.reshape(1, count),
        bricks.reshape(count, rows, extent),
    )

    def move(what, step):
        return lax.ppermute(what, "gz", [(z, (z + step) % planes) for z in range(planes)])

    def pick(parts, blocks, per=None):
        per = per or 1 + max(place for place, _ in parts)
        total = sum(b.shape[0] for b in blocks)
        return pl.pallas_call(
            lambda *refs: pick_kernel(parts, *refs, per=per),
            name="pick",
            out_shape=jax.ShapeDtypeStruct((columns * per, rows + META, extent), BF16),
            in_specs=[vmem] * len(blocks),
            out_specs=vmem,
            scratch_shapes=[
                VMEM((total, 128), jnp.int32),
                SMEM((total, 128), jnp.int32),
                pltpu.SemaphoreType.DMA,
            ],
            cost_estimate=pl.CostEstimate(flops=0, bytes_accessed=6_000_000, transcendentals=0),
        )(*blocks)

    def add(send, place, block):
        per = send.shape[0] // columns
        return pl.pallas_call(
            lambda *refs: add_kernel(place, per, *refs),
            name="add",
            out_shape=jax.ShapeDtypeStruct(send.shape, BF16),
            in_specs=[vmem, here],
            out_specs=here,
            input_output_aliases={1: 0},
            scratch_shapes=[
                VMEM((columns, rows + META, extent), BF16),
                VMEM((count, 128), jnp.int32),
                SMEM((count, 128), jnp.int32),
                pltpu.SemaphoreType.DMA,
                pltpu.SemaphoreType.DMA((columns,)),
            ],
        )(block, send)

    def spread(what):
        return lax.all_to_all(what, "gy", split_axis=0, concat_axis=0, tiled=True)

    def render(recv):
        slots = recv.shape[0]
        return pl.pallas_call(
            render_kernel,
            name="render",
            out_shape=jax.ShapeDtypeStruct((slots, 4, extent, extent), BF16),
            in_specs=[smem] * 3 + [vmem],
            out_specs=vmem,
            scratch_shapes=tables + small + [pltpu.SemaphoreType.DMA((2,))],
            compiler_params=pltpu.CompilerParams(vmem_limit_bytes=67_043_328),
            cost_estimate=pl.CostEstimate(flops=0, bytes_accessed=8_000_000, transcendentals=0),
        )(shear.T, color_gain, color_bias, recv)

    ups, downs = [block], [block]
    for _ in range(1, planes // 2):
        ups.append(move(ups[-1], 1))
        downs.append(move(downs[-1], -1))
    far = move(ups[-1], 1)

    groups = (
        (((0, 0),), (block,)),
        (((0, 0), (1, 0)), (ups[1], downs[1])),
        (((0, 0), (1, 0)), (ups[2], downs[2])),
        (((0, 0), (1, 0)), (ups[3], downs[3])),
    )
    received = []
    for at, (parts, blocks) in enumerate(groups):
        send = pick(parts, blocks, 3 if at == 3 else None)
        if at == 3:
            send = add(send, 2, far)
        received.append(spread(send))
    slots = sum(r.shape[0] for r in received)
    middle = []
    for recv in received[:-1]:
        middle += [recv, render(recv)]
    return pl.pallas_call(
        paint_kernel,
        name="paint",
        out_shape=jax.ShapeDtypeStruct((2, 4, extent, extent), F32),
        in_specs=[smem] * 3 + [here] * (len(middle) + 1),
        out_specs=vmem,
        scratch_shapes=[VMEM((slots, 4, extent, extent), BF16)]
        + tables
        + [
            VMEM((slots, META, 128), BF16),
            VMEM(received[-1].shape, BF16),
            VMEM((8, 128), jnp.int32),
            SMEM((8, 128), jnp.int32),
        ]
        + small
        + [pltpu.SemaphoreType.DMA((5 + len(middle),))],
    )(shear.T, color_gain, color_bias, *middle, received[-1])


def solution(mesh):
    whole = ("gx", "gy", "gz")
    placed = (
        P(whole, None, None, None),
        P(whole),
        P(),
        P(whole, None, None),
        P(whole),
        P(),
        P(),
        P(whole, None),
        P(None, whole),
    )

    return jax.shard_map(
        body,
        mesh=mesh,
        in_specs=placed,
        out_specs=P(whole, None, None, None),
        check_vma=False,
    )
```
